32 devices in a mesh: axial: 8 (over y, x, core), theta: 4 (over z).
Axes of the slice: x: 2, y: 2, z: 4, core: 2. Of those that a mesh axis runs over, the one named last changes fastest.
Arguments:
- rhs_field: float32 [16, 16, 32, 320], P('theta', 'axial'), may hold values from -6 to 6
- diag_inv: float32 [16, 16, 320, 320], P('theta', 'axial'), may hold values from -0.5 to 2
- lower_block: float32 [16, 16, 320, 320], P('theta', 'axial'), may hold values from -2 to 0.5
- upper_block: float32 [16, 16, 320, 320], P('theta', 'axial'), may hold values from -2 to 0.5
- proj_table: float32 [16, 80, 80], replicated, may hold values from -0.5 to 0.5
- intersection_list: int32 [16, 2], P('theta'), may hold values from 0 to 15
- proj_index: int32 [16, 2], P('theta'), may hold values from 0 to 15
- angle_step: int32 [1], replicated, may hold values from 0 to 15
Outputs:
- solution: float32 [16, 16, 32, 320], P('theta', 'axial')
- mortar: float32 [8, 16, 2560], P('axial', 'theta')
The draws below stay inside these ranges and needn't reach their ends.
All inputs are finite; a program needn't handle non-finite values.
Results may differ from the reference program's by a relative error of at most 0.0002.
Values sent between devices are 32-bit elements; how exact they have to be, the bound alone decides.
No kernel may reach another device: no remote copies, remote signals or barrier semaphores. Data moves between devices by JAX's collectives and lax.ppermute only.
A program may use at most 64 MiB of HBM per device.

```python
import math
import jax
import jax.numpy as jnp
from jax import lax

B = 320
FACE = 80
ELEM_DEV = 2
VECS = 32
NPROJ = 16
INTERSECTIONS = 2
ELEMENTS_PER_LINE = 16
LINE_COUNT_TOTAL = 16
N_AXIAL = 8


def line_rates(key, salt_value):
    base_key = jax.random.fold_in(key, salt_value)
    random_keys = jax.random.split(base_key, 5)
    slow_share = 0.5
    slow_mask = jax.random.uniform(random_keys[0], (LINE_COUNT_TOTAL, B)) < slow_share
    slow_rate = jax.random.uniform(random_keys[1], (LINE_COUNT_TOTAL, B), minval=0.9, maxval=0.96)
    fast_rate = jnp.exp(jax.random.uniform(random_keys[2], (LINE_COUNT_TOTAL, B), minval=math.log(0.05), maxval=math.log(0.5)))
    base_rate = jnp.where(slow_mask, slow_rate, fast_rate)
    jitter = jax.random.uniform(random_keys[3], (LINE_COUNT_TOTAL, ELEMENTS_PER_LINE, B), minval=0.98, maxval=1.02)
    surge_events = jax.random.randint(random_keys[4], (LINE_COUNT_TOTAL, 3), 0, ELEMENTS_PER_LINE)
    element_numbers = jnp.arange(ELEMENTS_PER_LINE, dtype=jnp.int32)
    surge_flag = jnp.any(surge_events[:, None, :] == element_numbers[None, :, None], axis=-1)
    sweep_rates = jnp.minimum(base_rate[:, None, :] * jitter, 0.97)
    return sweep_rates * jnp.where(surge_flag[:, :, None], 0.6, 1.0)


def diag_scale(key):
    return jnp.exp(jax.random.uniform(jax.random.fold_in(key, 11), (LINE_COUNT_TOTAL, ELEMENTS_PER_LINE, B), minval=math.log(0.7), maxval=math.log(1.4)))


def block_noise(key, salt_value):
    noise = jax.random.normal(jax.random.fold_in(key, salt_value), (LINE_COUNT_TOTAL, ELEMENTS_PER_LINE, B, B), jnp.float32)
    return jnp.clip(noise, -4.0, 4.0) * (0.2 / math.sqrt(B))


def draw_diag_inv(key, part):
    scales = diag_scale(key)
    identity = jnp.eye(B, dtype=jnp.float32)
    return scales[..., None] * identity + block_noise(key, 21) * scales[..., None]


def draw_lower_block(key, part):
    ratio = line_rates(key, 31) / diag_scale(key)
    identity = jnp.eye(B, dtype=jnp.float32)
    return -(ratio[..., None] * identity + block_noise(key, 41) * ratio[..., None])


def draw_upper_block(key, part):
    ratio = line_rates(key, 51) / diag_scale(key)
    identity = jnp.eye(B, dtype=jnp.float32)
    return -(ratio[..., None] * identity + block_noise(key, 61) * ratio[..., None])


def touch_ends(values, stream_key, least, largest):
    place = [jax.random.randint(jax.random.fold_in(stream_key, axis), (), 0, length) for axis, length in enumerate(values.shape)]
    main_axis = values.shape.index(max(values.shape))
    neighbour = place[:main_axis] + [(place[main_axis] + 1) % values.shape[main_axis]] + place[main_axis + 1:]
    return values.at[tuple(place)].set(least).at[tuple(neighbour)].set(largest)


def block_scale(stream_key, shape, shards, low, high):
    gain = 1.0
    for dim, shards_of in shards:
        heights = jax.random.uniform(jax.random.fold_in(jax.random.fold_in(stream_key, 6), dim), (shards_of,), jnp.float32, low / len(shards), high / len(shards))
        gain = gain * jnp.repeat(jnp.exp(heights), shape[dim] // shards_of).reshape((-1,) + (1,) * (len(shape) - 1 - dim))
    return gain


def normal_values(key, extent, width, bound, cuts=(), kind=jnp.bfloat16):
    level = block_scale(key, extent, cuts, -0.22, 0.18) if cuts else 1.0
    array = jax.random.normal(key, extent, jnp.float32) * width * level
    return jnp.minimum(jnp.maximum(array, -bound), bound).astype(kind)


def setup_inputs(seed: int = 0) -> dict:
    splits = jax.random.split(jax.random.key(seed), 9)
    rhs_field = normal_values(splits[0], (LINE_COUNT_TOTAL, ELEMENTS_PER_LINE, VECS, B), 1.0, 6.0, ((0, 4), (1, 8)), jnp.float32)
    diag_inv = draw_diag_inv(jax.random.fold_in(splits[8], 71), 0)
    lower_block = draw_lower_block(jax.random.fold_in(splits[8], 71), 0)
    upper_block = draw_upper_block(jax.random.fold_in(splits[8], 71), 0)
    proj_table = normal_values(splits[4], (NPROJ, FACE, FACE), (2 * FACE) ** -0.5, 0.5, (), jnp.float32)
    intersection_list = touch_ends(jax.random.randint(splits[5], (LINE_COUNT_TOTAL, INTERSECTIONS), 0, LINE_COUNT_TOTAL), jax.random.fold_in(splits[5], 1), 0, LINE_COUNT_TOTAL - 1).astype(jnp.int32)
    proj_index = touch_ends(jax.random.randint(splits[6], (LINE_COUNT_TOTAL, INTERSECTIONS), 0, NPROJ), jax.random.fold_in(splits[6], 1), 0, NPROJ - 1).astype(jnp.int32)
    angle_step = jax.random.randint(splits[7], (1,), 0, LINE_COUNT_TOTAL).astype(jnp.int32)
    return dict(rhs_field=rhs_field, diag_inv=diag_inv, lower_block=lower_block, upper_block=upper_block, proj_table=proj_table, intersection_list=intersection_list, proj_index=proj_index, angle_step=angle_step)


def product(blocks, vectors):
    return jnp.einsum('lbc,lvc->lvb', blocks, vectors, precision=lax.Precision.HIGHEST)


def reference(rhs_field, diag_inv, lower_block, upper_block, proj_table, intersection_list, proj_index, angle_step):
    def select_element(source, element):
        return lax.dynamic_index_in_dim(source, element, 1, keepdims=False)

    def forward(previous, element):
        inner = select_element(rhs_field, element) - product(select_element(lower_block, element), previous)
        current = product(select_element(diag_inv, element), inner)
        return current, current

    zero_state = jnp.zeros((LINE_COUNT_TOTAL, VECS, B), jnp.float32)
    element_numbers = jnp.arange(ELEMENTS_PER_LINE, dtype=jnp.int32)
    _, swept = lax.scan(forward, zero_state, element_numbers)

    def backward(following, element):
        coupled = product(select_element(upper_block, element), following)
        current = lax.dynamic_index_in_dim(swept, element, 0, keepdims=False) - product(select_element(diag_inv, element), coupled)
        return current, current

    _, solved = lax.scan(backward, zero_state, element_numbers, reverse=True)
    solution = jnp.transpose(solved, (1, 0, 2, 3))
    traces = solution[:, ELEM_DEV - 1::ELEM_DEV, :, B - FACE:]
    sources = ((intersection_list + angle_step[0]) % LINE_COUNT_TOTAL).astype(jnp.int32)
    picked = traces[sources]
    one_hot = jax.nn.one_hot(proj_index, NPROJ, dtype=jnp.float32)
    chosen = jnp.einsum('gkp,pfh->gkfh', one_hot, proj_table, precision=lax.Precision.HIGHEST)
    mortar = jnp.einsum('gkfh,gkavh->agvf', chosen, picked, precision=lax.Precision.HIGHEST)
    return solution, mortar.reshape(N_AXIAL, LINE_COUNT_TOTAL, VECS * FACE)
```

```python
import jax
import jax.numpy as jnp
from jax import lax
from jax.sharding import PartitionSpec as P

HIGH = lax.Precision.HIGH


def apply(blocks, vectors):
    return jnp.einsum("lbc,lvc->lvb", blocks, vectors, precision=HIGH)


def compose(left, right):
    return jnp.einsum("lbc,lcd->lbd", left, right, precision=HIGH)


def local(
    rhs_field,
    diag_inv,
    lower_block,
    upper_block,
    proj_table,
    intersection_list,
    proj_index,
    angle_step,
):
    lines, elems, vecs, size = rhs_field.shape
    devices = lax.axis_size("axial")
    chips = devices // 2
    half = lines // 2
    core = lax.axis_index("axial") % 2
    partner = [(d, d ^ 1) for d in range(devices)]

    def owned(value):
        mine = lax.dynamic_slice_in_dim(value, core * half, half, 0)
        other = lax.dynamic_slice_in_dim(value, (1 - core) * half, half, 0)
        got = lax.ppermute(other, "axial", partner)
        first = jnp.where(core == 0, mine, got)
        second = jnp.where(core == 0, got, mine)
        return jnp.concatenate([first, second], axis=1)

    def disowned(value):
        mine = lax.dynamic_slice_in_dim(value, core * elems, elems, 1)
        other = lax.dynamic_slice_in_dim(value, (1 - core) * elems, elems, 1)
        got = lax.ppermute(other, "axial", partner)
        first = jnp.where(core == 0, mine, got)
        second = jnp.where(core == 0, got, mine)
        return jnp.concatenate([first, second], axis=0)

    scaled = jnp.einsum("lebc,levc->levb", diag_inv, rhs_field, precision=HIGH)
    down = jnp.einsum("lebc,lecd->lebd", diag_inv, lower_block, precision=HIGH)
    up = jnp.einsum("lebc,lecd->lebd", diag_inv, upper_block, precision=HIGH)
    scaled, down = owned(scaled), owned(down)
    up = owned(up)
    count = 2 * elems

    parts = [scaled[:, 0]]
    maps = [-down[:, 0]]
    for e in range(1, count):
        parts.append(scaled[:, e] - apply(down[:, e], parts[-1]))
        maps.append(-compose(down[:, e], maps[-1]))

    incoming = jnp.zeros_like(parts[0])
    outgoing = parts[-1]
    for k in range(chips - 1):
        hop = [(2 * k + c, 2 * k + 2 + c) for c in range(2)]
        got = lax.ppermute(outgoing, "axial", hop)
        incoming = incoming + got
        outgoing = parts[-1] + apply(maps[-1], got)
    swept = [p + apply(m, incoming) for p, m in zip(parts, maps)]

    parts = [None] * count
    maps = [None] * count
    parts[-1] = swept[-1]
    maps[-1] = -up[:, -1]
    for e in reversed(range(count - 1)):
        parts[e] = swept[e] - apply(up[:, e], parts[e + 1])
        maps[e] = -compose(up[:, e], maps[e + 1])

    incoming = jnp.zeros_like(parts[0])
    outgoing = parts[0]
    for k in reversed(range(1, chips)):
        hop = [(2 * k + c, 2 * k - 2 + c) for c in range(2)]
        got = lax.ppermute(outgoing, "axial", hop)
        incoming = incoming + got
        outgoing = parts[0] + apply(maps[0], got)
    solved = jnp.stack([p + apply(m, incoming) for p, m in zip(parts, maps)], axis=1)
    solution = disowned(solved)

    face = proj_table.shape[1]
    traces = solution[:, -1, :, size - face :]
    groups = lax.axis_size("theta")
    here = lax.axis_index("theta")
    sources = (intersection_list + angle_step[0]) % (lines * groups)
    owner, place = sources // lines, sources % lines
    row_ids = jnp.arange(lines, dtype=jnp.int32)
    picked = 0.0
    for shift in range(groups):
        if shift:
            ring = [(t, (t + shift) % groups) for t in range(groups)]
            block = lax.ppermute(traces, "theta", ring)
        else:
            block = traces
        take = (owner == (here - shift) % groups)[:, :, None] & (
            place[:, :, None] == row_ids
        )
        picked = picked + jnp.einsum(
            "gkn,nvh->gkvh", take.astype(jnp.float32), block, precision=lax.Precision.HIGHEST
        )
    one_hot = jax.nn.one_hot(proj_index, proj_table.shape[0], dtype=jnp.float32)
    chosen = jnp.einsum("gkp,pfh->gkfh", one_hot, proj_table, precision=lax.Precision.HIGHEST)
    mortar = jnp.einsum("gkfh,gkvh->gvf", chosen, picked, precision=HIGH)
    return (solution, mortar.reshape(1, lines, vecs * face))


def solution(mesh):
    block = P("theta", "axial", None, None)
    return jax.shard_map(
        local,
        mesh=mesh,
        in_specs=(block, block, block, block, P(), P("theta", None), P("theta", None), P()),
        out_specs=(block, P("axial", "theta", None)),
        check_vma=False,
    )
```

```python
import jax
import jax.numpy as jnp
from jax import lax
from jax.experimental import pallas as pl
from jax.experimental.pallas import tpu as pltpu
from jax.sharding import PartitionSpec as P


F32 = jnp.float32
BF16 = jnp.bfloat16
PLAIN = (((1,), (0,)), ((), ()))
RIGHT_T = (((1,), (1,)), ((), ()))
BOTH_T = (((0,), (1,)), ((), ()))
VMEM = pl.BlockSpec(memory_space=pltpu.VMEM)
SMEM = pl.BlockSpec(memory_space=pltpu.SMEM)
LIMIT = 12 << 20


def dot(a, b, dims=PLAIN):
    return lax.dot_general(a, b, dims, preferred_element_type=F32)


def split(a):
    high = a.astype(BF16)
    return high, (a - high.astype(F32)).astype(BF16)


def dot3(a, b, dims=PLAIN):
    ah, al = a
    bh, bl = b
    return dot(ah, bh, dims) + (dot(ah, bl, dims) + dot(al, bh, dims))


def rows(vectors, high, low):
    count = vectors.shape[0]
    vh, vl = split(vectors)
    both = dot(jnp.concatenate([vh, vl], axis=0), high)
    return both[:count] + (both[count:] + dot(vh, low))


def call(kernel, out_shape, in_specs, out_specs, flops=0, **kwargs):
    return pl.pallas_call(
        kernel,
        out_shape=out_shape,
        in_specs=in_specs,
        out_specs=out_specs,
        compiler_params=pltpu.CompilerParams(vmem_limit_bytes=LIMIT),
        cost_estimate=pl.CostEstimate(flops=flops, bytes_accessed=0, transcendentals=0),
        **kwargs,
    )


def struct(*shape, dtype=F32):
    return pltpu.VMEM(shape, dtype)


def product_of(left, right, left_stage, right_stage, slot):
    size = left.shape[0]
    high, low = split(left)
    left_stage[slot, :, :size] = high
    left_stage[slot, :, size : 2 * size] = high
    left_stage[slot, :, 2 * size :] = low
    high, low = split(right)
    right_stage[slot, :size] = high
    right_stage[slot, size : 2 * size] = low
    right_stage[slot, 2 * size :] = high
    return -dot(right_stage[slot], left_stage[slot], BOTH_T)


def stages(size):
    return [pltpu.VMEM((2, size, 3 * size), BF16), pltpu.VMEM((2, 3 * size, size), BF16)]


def scaled_rhs(rhs, left_stage, slot):
    high, low = split(rhs)
    return dot(jnp.concatenate([high, low, high], axis=1), left_stage[slot], RIGHT_T)


def first_products(left, right, rhs, flops):
    lines, elems, size, _ = left.shape
    half = lines // 2
    vecs = rhs.shape[2]
    matrix = (half, elems, size, size)
    column = (half, elems, vecs, size)

    def kernel(
        left_hbm, right_hbm, rhs_hbm,
        out_ref, out_g, left_other, left_mine, right_mine, rhs_mine,
        right_other, rhs_other, left_stage, right_stage, sems, rhs_sems,
    ):
        core = core_index()
        mine, other = core * half, (1 - core) * half
        places = [(n, e) for n in range(half) for e in range(elems)]

        def pair(base, left_ref, right_ref, group, n, e):
            index = n * elems + e
            return (
                pltpu.make_async_copy(
                    left_hbm.at[base + n, e], left_ref.at[n, e], sems.at[group, 0, index]
                ),
                pltpu.make_async_copy(
                    right_hbm.at[base + n, e], right_ref.at[n, e], sems.at[group, 1, index]
                ),
            )

        near = [pair(other, left_other, right_other, 0, n, e) for n, e in places]
        far = [pair(mine, left_mine, right_mine, 1, n, e) for n, e in places]
        rhs_near = pltpu.make_async_copy(rhs_hbm.at[pl.ds(other, half)], rhs_other, rhs_sems.at[0])
        rhs_far = pltpu.make_async_copy(rhs_hbm.at[pl.ds(mine, half)], rhs_mine, rhs_sems.at[1])
        for index, copies in enumerate(near):
            for copy in copies:
                copy.start()
            if index == 0:
                rhs_near.start()
        rhs_far.start()
        for index, (n, e) in enumerate(places):
            for copy in near[index]:
                copy.wait()
            for copy in far[index]:
                copy.start()
            if index == 0:
                rhs_near.wait()
            slot = index % 2
            out_ref[n, e] = product_of(
                left_other[n, e], right_other[n, e], left_stage, right_stage, slot
            )
            out_g[n, e] = scaled_rhs(rhs_other[n, e], left_stage, slot)
        for copies in far:
            for copy in copies:
                copy.wait()
        rhs_far.wait()

    hbm = [pltpu.with_memory_space_constraint(x, pltpu.HBM) for x in (left, right, rhs)]
    return call(
        kernel,
        [struct(*shape) for shape in (matrix, column, matrix, matrix, matrix, column)],
        [pl.BlockSpec(memory_space=pltpu.HBM)] * 3,
        [VMEM] * 6,
        flops,
        scratch_shapes=[
            pltpu.VMEM(matrix, F32),
            pltpu.VMEM(column, F32),
            *stages(size),
            pltpu.SemaphoreType.DMA((2, 2, half * elems)),
            pltpu.SemaphoreType.DMA((2,)),
        ],
    )(*hbm)


def second_products(left, right, rhs, later, flops):
    half, elems, size, _ = left.shape

    def kernel(
        left_ref, right_ref, rhs_ref, later_hbm,
        out_ref, out_g, later_other, later_mine, left_stage, right_stage, sems,
    ):
        core = core_index()
        copies = [
            pltpu.make_async_copy(later_hbm.at[pl.ds(base, half)], target, sems.at[index])
            for index, (base, target) in enumerate(
                (((1 - core) * half, later_other), (core * half, later_mine))
            )
        ]
        for copy in copies:
            copy.start()
        for n in range(half):
            for e in range(elems):
                slot = (n * elems + e) % 2
                out_ref[n, e] = product_of(
                    left_ref[n, e], right_ref[n, e], left_stage, right_stage, slot
                )
                out_g[n, e] = scaled_rhs(rhs_ref[n, e], left_stage, slot)
        for copy in copies:
            copy.wait()

    return call(
        kernel,
        [struct(*shape) for shape in (left.shape, rhs.shape, left.shape, left.shape)],
        [VMEM] * 3 + [pl.BlockSpec(memory_space=pltpu.HBM)],
        [VMEM] * 4,
        flops,
        scratch_shapes=[*stages(size), pltpu.SemaphoreType.DMA((2,))],
    )(left, right, rhs, pltpu.with_memory_space_constraint(later, pltpu.HBM))


def late_products(left, right, flops):
    half, elems, size, _ = left.shape

    def kernel(left_ref, right_ref, out_ref, left_stage, right_stage):
        for n in range(half):
            for e in range(elems):
                slot = (n * elems + e) % 2
                out_ref[n, e] = product_of(
                    left_ref[n, e], right_ref[n, e], left_stage, right_stage, slot
                )

    return call(
        kernel, struct(*left.shape), [VMEM] * 2, VMEM, flops, scratch_shapes=stages(size)
    )(left, right)


def composed(high, low, order, flops):
    half, _, size, _ = high.shape

    def kernel(high_ref, low_ref, out_high, out_low, left_stage, right_stage):
        for n in range(half):
            out_high[n, order[0]] = high_ref[n, order[0]]
            out_low[n, order[0]] = low_ref[n, order[0]]
        for before, e in zip(order, order[1:]):
            for n in range(half):
                h, l = out_high[n, before], out_low[n, before]
                left_stage[n, :, :size] = h
                left_stage[n, :, size : 2 * size] = h
                left_stage[n, :, 2 * size :] = l
                right_stage[n, :size] = high_ref[n, e]
                right_stage[n, size : 2 * size] = low_ref[n, e]
                right_stage[n, 2 * size :] = high_ref[n, e]
                h, l = split(dot(left_stage[n], right_stage[n]))
                out_high[n, e] = h
                out_low[n, e] = l

    shape = struct(*high.shape, dtype=BF16)
    return call(
        kernel,
        [shape, shape],
        [VMEM] * 2,
        [VMEM] * 2,
        flops,
        scratch_shapes=[
            pltpu.VMEM((half, size, 3 * size), BF16),
            pltpu.VMEM((half, 3 * size, size), BF16),
        ],
    )(high, low)


def core_index():
    return lax.rem(lax.axis_index("axial"), 2)


def ordered(mine_ref, got_ref, high_ref, low_ref):
    count, elems, _, _ = mine_ref.shape
    core = core_index()
    for source, first in ((mine_ref, core * elems), (got_ref, (1 - core) * elems)):
        for n in range(count):
            for e in range(elems):
                high, low = split(source[n, e])
                high_ref[n, first + e] = high
                low_ref[n, first + e] = low


def local(
    rhs_field,
    diag_inv,
    lower_block,
    upper_block,
    proj_table,
    intersection_list,
    proj_index,
    angle_step,
):
    lines, elems, vecs, size = rhs_field.shape
    devices = lax.axis_size("axial")
    chips = devices // 2
    half = lines // 2
    total = 2 * elems
    partner = [(d, d ^ 1) for d in range(devices)]
    stack = struct(half, total, size, size, dtype=BF16)
    field = struct(half, total, vecs, size)
    edge = struct(half, vecs, size)
    work = half * total * 6 * vecs * size**2

    heavy = half * elems * 6 * size**3
    other_p, other_g, d_other, d_mine, l_mine, r_mine = first_products(
        diag_inv, lower_block, rhs_field, heavy
    )
    got_p = lax.ppermute(other_p, "axial", partner)
    got_g = lax.ppermute(other_g, "axial", partner)
    mine_p, mine_g, u_other, u_mine = second_products(d_mine, l_mine, r_mine, upper_block, heavy)

    def start_kernel(mine_ref, got_ref, mg_ref, gg_ref, high_ref, low_ref, part_ref):
        ordered(mine_ref, got_ref, high_ref, low_ref)
        core = core_index()
        for source, first in ((mg_ref, core * elems), (gg_ref, (1 - core) * elems)):
            for n in range(half):
                for e in range(elems):
                    part_ref[n, first + e] = source[n, e]
        for n in range(half):
            current = part_ref[n, 0]
            for e in range(1, total):
                current = part_ref[n, e] + rows(current, high_ref[n, e], low_ref[n, e])
                part_ref[n, e] = current

    p_high, p_low, parts = call(
        start_kernel, (stack, stack, field), [VMEM] * 4, (VMEM,) * 3, work
    )(mine_p, got_p, mine_g, got_g)
    outgoing = parts[:, -1]

    x_high, x_low = composed(p_high, p_low, list(range(total)), 2 * heavy)

    def hop_kernel(edge_at):
        def kernel(in_ref, high_ref, low_ref, part_ref, out_ref):
            for n in range(half):
                out_ref[n] = part_ref[n, edge_at] + rows(
                    in_ref[n], high_ref[n, edge_at], low_ref[n, edge_at]
                )

        return kernel

    incoming = jnp.zeros_like(outgoing)
    for k in range(chips - 1):
        got = lax.ppermute(outgoing, "axial", [(2 * k + c, 2 * k + 2 + c) for c in range(2)])
        incoming = incoming + got
        if k < chips - 2:
            outgoing = call(hop_kernel(total - 1), edge, [VMEM] * 4, VMEM, work // total)(
                got, x_high, x_low, parts
            )

    other_q = late_products(d_other, u_other, heavy)
    got_q = lax.ppermute(other_q, "axial", partner)
    mine_q = late_products(d_mine, u_mine, heavy)

    q_high, q_low = call(ordered, (stack, stack), [VMEM] * 2, (VMEM,) * 2)(mine_q, got_q)

    def turn_kernel(in_ref, xh_ref, xl_ref, part_ref, qh_ref, ql_ref, back_ref):
        for n in range(half):
            for e in range(total):
                back_ref[n, e] = part_ref[n, e] + rows(in_ref[n], xh_ref[n, e], xl_ref[n, e])
        for n in range(half):
            current = back_ref[n, total - 1]
            for e in reversed(range(total - 1)):
                current = back_ref[n, e] + rows(current, qh_ref[n, e], ql_ref[n, e])
                back_ref[n, e] = current

    backs = call(turn_kernel, field, [VMEM] * 6, VMEM, 2 * work)(
        incoming, x_high, x_low, parts, q_high, q_low
    )
    outgoing = backs[:, 0]

    y_high, y_low = composed(q_high, q_low, list(range(total))[::-1], 2 * heavy)

    incoming = jnp.zeros_like(outgoing)
    for k in reversed(range(1, chips)):
        got = lax.ppermute(outgoing, "axial", [(2 * k + c, 2 * k - 2 + c) for c in range(2)])
        incoming = incoming + got
        if k > 1:
            outgoing = call(hop_kernel(0), edge, [VMEM] * 4, VMEM, work // total)(
                got, y_high, y_low, backs
            )

    def last_kernel(in_ref, high_ref, low_ref, part_ref, mine_ref, other_ref, all_ref):
        for n in range(half):
            for e in range(total):
                all_ref[n, e] = part_ref[n, e] + rows(in_ref[n], high_ref[n, e], low_ref[n, e])
        first = core_index() * elems
        away = (1 - core_index()) * elems
        for n in range(half):
            for e in range(elems):
                mine_ref[n, e] = all_ref[n, first + e]
                other_ref[n, e] = all_ref[n, away + e]

    part = struct(half, elems, vecs, size)
    mine_z, other_z = call(
        last_kernel,
        (part, part),
        [VMEM] * 4,
        (VMEM,) * 2,
        work,
        scratch_shapes=[pltpu.VMEM(field.shape, F32)],
    )(incoming, y_high, y_low, backs)
    got_z = lax.ppermute(other_z, "axial", partner)

    face = proj_table.shape[1]

    def join_kernel(mine_ref, got_ref, field_ref, trace_ref):
        core = core_index()
        for source, base in ((mine_ref, core * half), (got_ref, (1 - core) * half)):
            for n in range(half):
                field_ref[base + n] = source[n]
                trace_ref[base + n] = source[n, elems - 1, :, size - face :]

    solution, traces = call(
        join_kernel,
        (jax.ShapeDtypeStruct(rhs_field.shape, F32), struct(lines, vecs, face)),
        [VMEM] * 2,
        (VMEM,) * 2,
    )(mine_z, got_z)

    groups = lax.axis_size("theta")
    blocks = [traces] + [
        lax.ppermute(traces, "theta", [(t, (t + s) % groups) for t in range(groups)])
        for s in range(1, groups)
    ]
    crossings = intersection_list.shape[1]

    def mortar_kernel(list_ref, index_ref, angle_ref, table_ref, *rest):
        out_ref = rest[-1]
        here = lax.axis_index("theta")
        for g in range(lines):
            sums = jnp.zeros((vecs, face), F32)
            for k in range(crossings):
                face_id = lax.rem(list_ref[g, k] + angle_ref[0], lines * groups)
                shift = lax.rem(here - lax.div(face_id, lines) + groups, groups)
                line = lax.rem(face_id, lines)
                trace = rest[0][line]
                for s in range(1, groups):
                    trace = jnp.where(shift == s, rest[s][line], trace)
                sums = sums + dot3(split(trace), split(table_ref[index_ref[g, k]]), RIGHT_T)
            out_ref[g] = sums

    mortar = call(
        mortar_kernel, jax.ShapeDtypeStruct((lines, vecs, face), F32), [SMEM] * 3 + [VMEM] * (1 + groups), VMEM
    )(intersection_list, proj_index, angle_step, proj_table, *blocks)
    return (solution, mortar.reshape(1, lines, vecs * face))


def solution(mesh):
    block = P("theta", "axial", None, None)
    return jax.shard_map(
        local,
        mesh=mesh,
        in_specs=(block, block, block, block, P(), P("theta", None), P("theta", None), P()),
        out_specs=(block, P("axial", "theta", None)),
        check_vma=False,
    )
```

```python
import jax
import jax.numpy as jnp
from jax import lax
from jax.experimental import pallas as pl
from jax.experimental.pallas import tpu as pltpu
from jax.sharding import PartitionSpec as P


F32 = jnp.float32
BF16 = jnp.bfloat16
PLAIN = (((1,), (0,)), ((), ()))
RIGHT_T = (((1,), (1,)), ((), ()))
BOTH_T = (((0,), (1,)), ((), ()))
VMEM = pl.BlockSpec(memory_space=pltpu.VMEM)
SMEM = pl.BlockSpec(memory_space=pltpu.SMEM)
LIMIT = 12 << 20


def dot(a, b, dims=PLAIN):
    return lax.dot_general(a, b, dims, preferred_element_type=F32)


def split(a):
    high = a.astype(BF16)
    return high, (a - high.astype(F32)).astype(BF16)


def dot3(a, b, dims=PLAIN):
    ah, al = a
    bh, bl = b
    return dot(ah, bh, dims) + (dot(ah, bl, dims) + dot(al, bh, dims))


def rows(vectors, high, low):
    count = vectors.shape[0]
    vh, vl = split(vectors)
    both = dot(jnp.concatenate([vh, vl], axis=0), high)
    return both[:count] + (both[count:] + dot(vh, low))


def call(kernel, out_shape, in_specs, out_specs, flops=0, **kwargs):
    return pl.pallas_call(
        kernel,
        out_shape=out_shape,
        in_specs=in_specs,
        out_specs=out_specs,
        compiler_params=pltpu.CompilerParams(vmem_limit_bytes=LIMIT),
        cost_estimate=pl.CostEstimate(flops=flops, bytes_accessed=0, transcendentals=0),
        **kwargs,
    )


def struct(*shape, dtype=F32):
    return pltpu.VMEM(shape, dtype)


def product_of(left, right, left_stage, right_stage, slot):
    size, width = right.shape
    high, low = split(left)
    left_stage[slot, :, :size] = high
    left_stage[slot, :, size : 2 * size] = high
    left_stage[slot, :, 2 * size :] = low
    high, low = split(right)
    right_stage[slot, :size, :width] = high
    right_stage[slot, size : 2 * size, :width] = low
    right_stage[slot, 2 * size :, :width] = high
    return dot(right_stage[slot, :, :width], left_stage[slot], BOTH_T)


def stages(size, width):
    return [pltpu.VMEM((2, size, 3 * size), BF16), pltpu.VMEM((2, 3 * size, width), BF16)]


def products(left_ref, right_ref, rhs_ref, out_ref, out_g, left_stage, right_stage):
    half, elems, _, _ = left_ref.shape
    for n in range(half):
        for e in range(elems):
            slot = (n * elems + e) % 2
            out_ref[n, e] = -product_of(
                left_ref[n, e], right_ref[n, e], left_stage, right_stage, slot
            )
            high, low = split(rhs_ref[n, e])
            terms = jnp.concatenate([high, low, high], axis=1)
            out_g[n, e] = dot(terms, left_stage[slot], RIGHT_T)


def first_products(left, right, rhs, flops):
    lines, elems, size, _ = left.shape
    half = lines // 2
    vecs = rhs.shape[2]
    matrix = (half, elems, size, size)
    column = (half, elems, vecs, size)

    def kernel(
        left_hbm, right_hbm, rhs_hbm,
        out_ref, out_g, left_other, left_mine, right_mine, rhs_mine,
        right_other, rhs_other, left_stage, right_stage, sems,
    ):
        core = core_index()
        targets = ((left_other, right_other, rhs_other), (left_mine, right_mine, rhs_mine))
        near, far = (
            [
                pltpu.make_async_copy(
                    source.at[pl.ds(base * half, half)], target, sems.at[group, i]
                )
                for i, (source, target) in enumerate(zip((left_hbm, right_hbm, rhs_hbm), refs))
            ]
            for group, (base, refs) in enumerate(zip((1 - core, core), targets))
        )
        for copy in near + far:
            copy.start()
        for copy in near:
            copy.wait()
        products(left_other, right_other, rhs_other, out_ref, out_g, left_stage, right_stage)
        for copy in far:
            copy.wait()

    hbm = [pltpu.with_memory_space_constraint(x, pltpu.HBM) for x in (left, right, rhs)]
    return call(
        kernel,
        [struct(*shape) for shape in (matrix, column, matrix, matrix, matrix, column)],
        [pl.BlockSpec(memory_space=pltpu.HBM)] * 3,
        [VMEM] * 6,
        flops,
        scratch_shapes=[
            pltpu.VMEM(matrix, F32),
            pltpu.VMEM(column, F32),
            *stages(size, size),
            pltpu.SemaphoreType.DMA((2, 3)),
        ],
    )(*hbm)


def second_products(left, right, rhs, flops):
    size = left.shape[2]
    return call(
        products,
        [struct(*left.shape), struct(*rhs.shape)],
        [VMEM] * 3,
        [VMEM] * 2,
        flops,
        scratch_shapes=stages(size, size),
    )(left, right, rhs)


def late_products(left, right, flops):
    half, elems, size, _ = left.shape

    def kernel(left_ref, right_ref, out_ref, left_stage, right_stage):
        for n in range(half):
            for e in range(elems):
                slot = (n * elems + e) % 2
                out_ref[n, e] = -product_of(
                    left_ref[n, e], right_ref[n, e], left_stage, right_stage, slot
                )

    return call(
        kernel, struct(*left.shape), [VMEM] * 2, VMEM, flops, scratch_shapes=stages(size, size)
    )(left, right)


def stage_left(stage, n, start, count, high, low):
    size = high.shape[1]
    stage[n, start : start + count, :size] = high
    stage[n, start : start + count, size : 2 * size] = high
    stage[n, start : start + count, 2 * size :] = low


def stage_right(stage, n, high, low):
    size = high.shape[0]
    stage[n, :size] = high
    stage[n, size : 2 * size] = low
    stage[n, 2 * size :] = high


def composed(mine, got, order, flops, later=None):
    half, elems, size, _ = mine.shape

    def kernel(mine_ref, got_ref, *rest):
        copies = []
        if later is not None:
            later_hbm, *rest, sems = rest
            targets = rest[2:4]
            core = core_index()
            copies = [
                pltpu.make_async_copy(later_hbm.at[pl.ds(base * half, half)], target, sems.at[i])
                for i, (base, target) in enumerate(zip((1 - core, core), targets))
            ]
        out_high, out_low, *_, left_stage, right_stage = rest
        for copy in copies:
            copy.start()
        for n in range(half):
            first = pick(mine_ref, got_ref, n, order[0])
            out_high[n, order[0]], out_low[n, order[0]] = split(first)
        for before, e in zip(order, order[1:]):
            for n in range(half):
                stage_left(left_stage, n, 0, size, out_high[n, before], out_low[n, before])
                stage_right(right_stage, n, *split(pick(mine_ref, got_ref, n, e)))
                out_high[n, e], out_low[n, e] = split(dot(left_stage[n], right_stage[n]))
        for copy in copies:
            copy.wait()

    shapes = [struct(half, len(order), size, size, dtype=BF16)] * 2
    specs, operands = [VMEM] * 2, [mine, got]
    scratch = [
        pltpu.VMEM((half, size, 3 * size), BF16),
        pltpu.VMEM((half, 3 * size, size), BF16),
    ]
    if later is not None:
        shapes += [struct(half, elems, size, size)] * 2
        specs.append(pl.BlockSpec(memory_space=pltpu.HBM))
        operands.append(pltpu.with_memory_space_constraint(later, pltpu.HBM))
        scratch.append(pltpu.SemaphoreType.DMA((2,)))
    return call(
        kernel, shapes, specs, [VMEM] * len(shapes), flops, scratch_shapes=scratch
    )(*operands)


def turned(x_high, x_low, parts, mine, got, flops):
    half, total, size, _ = x_high.shape
    vecs = parts.shape[2]

    def kernel(
        xh_ref, xl_ref, part_ref, mine_ref, got_ref,
        out_high, out_low, out_part, left_stage, right_stage,
    ):
        last = total - 1
        for n in range(half):
            out_high[n, last] = xh_ref[n, last]
            out_low[n, last] = xl_ref[n, last]
            out_part[n, last] = part_ref[n, last]
        for e in reversed(range(last)):
            for n in range(half):
                stage_left(left_stage, n, 0, size, out_high[n, e + 1], out_low[n, e + 1])
                stage_left(left_stage, n, size, vecs, *split(out_part[n, e + 1]))
                stage_right(right_stage, n, *split(pick(mine_ref, got_ref, n, e)))
                result = dot(left_stage[n], right_stage[n])
                x = xh_ref[n, e].astype(F32) + xl_ref[n, e].astype(F32)
                out_high[n, e], out_low[n, e] = split(x + result[:size])
                out_part[n, e] = part_ref[n, e] + result[size:]

    shape = struct(*x_high.shape, dtype=BF16)
    return call(
        kernel,
        [shape, shape, struct(*parts.shape)],
        [VMEM] * 5,
        [VMEM] * 3,
        flops,
        scratch_shapes=[
            pltpu.VMEM((half, size + vecs, 3 * size), BF16),
            pltpu.VMEM((half, 3 * size, size), BF16),
        ],
    )(x_high, x_low, parts, mine, got)


def core_index():
    return lax.rem(lax.axis_index("axial"), 2)


def pick(mine_ref, got_ref, n, e):
    elems = mine_ref.shape[1]
    owner, place = divmod(e, elems)
    return jnp.where(core_index() == owner, mine_ref[n, place], got_ref[n, place])


def local(
    rhs_field,
    diag_inv,
    lower_block,
    upper_block,
    proj_table,
    intersection_list,
    proj_index,
    angle_step,
):
    lines, elems, vecs, size = rhs_field.shape
    devices = lax.axis_size("axial")
    chips = devices // 2
    half = lines // 2
    total = 2 * elems
    partner = [(d, d ^ 1) for d in range(devices)]
    field = struct(half, total, vecs, size)
    edge = struct(half, vecs, size)
    work = half * total * 6 * vecs * size**2

    heavy = half * elems * 6 * size**3
    other_p, other_g, d_other, d_mine, l_mine, r_mine = first_products(
        diag_inv, lower_block, rhs_field, heavy
    )
    got_p = lax.ppermute(other_p, "axial", partner)
    got_g = lax.ppermute(other_g, "axial", partner)
    mine_p, mine_g = second_products(d_mine, l_mine, r_mine, heavy)

    def start_kernel(mine_ref, got_ref, mine_g_ref, got_g_ref, part_ref):
        for n in range(half):
            current = pick(mine_g_ref, got_g_ref, n, 0)
            part_ref[n, 0] = current
            for e in range(1, total):
                operator = split(pick(mine_ref, got_ref, n, e))
                current = pick(mine_g_ref, got_g_ref, n, e) + rows(current, *operator)
                part_ref[n, e] = current

    parts = call(start_kernel, field, [VMEM] * 4, VMEM, work)(mine_p, got_p, mine_g, got_g)
    outgoing = parts[:, -1]

    x_high, x_low, u_other, u_mine = composed(
        mine_p, got_p, list(range(total)), 2 * heavy, upper_block
    )

    def hop_kernel(edge_at):
        def kernel(in_ref, high_ref, low_ref, part_ref, out_ref):
            for n in range(half):
                out_ref[n] = part_ref[n, edge_at] + rows(
                    in_ref[n], high_ref[n, edge_at], low_ref[n, edge_at]
                )

        return kernel

    incoming = jnp.zeros_like(outgoing)
    for k in range(chips - 1):
        got = lax.ppermute(outgoing, "axial", [(2 * k + c, 2 * k + 2 + c) for c in range(2)])
        incoming = incoming + got
        if k < chips - 2:
            outgoing = call(hop_kernel(total - 1), edge, [VMEM] * 4, VMEM, work // total)(
                got, x_high, x_low, parts
            )

    other_q = late_products(d_other, u_other, heavy)
    got_q = lax.ppermute(other_q, "axial", partner)
    mine_q = late_products(d_mine, u_mine, heavy)

    t_high, t_low, t_parts = turned(x_high, x_low, parts, mine_q, got_q, 2 * heavy)

    outgoing = call(hop_kernel(0), edge, [VMEM] * 4, VMEM, work // total)(
        incoming, t_high, t_low, t_parts
    )

    def all_kernel(in_ref, high_ref, low_ref, part_ref, out_ref):
        for n in range(half):
            for e in range(total):
                out_ref[n, e] = part_ref[n, e] + rows(in_ref[n], high_ref[n, e], low_ref[n, e])

    backs = call(all_kernel, field, [VMEM] * 4, VMEM, work)(
        incoming, t_high, t_low, t_parts
    )
    y_high, y_low = composed(mine_q, got_q, list(range(total))[::-1], 2 * heavy)

    incoming = jnp.zeros_like(outgoing)
    for k in reversed(range(1, chips)):
        got = lax.ppermute(outgoing, "axial", [(2 * k + c, 2 * k - 2 + c) for c in range(2)])
        incoming = incoming + got
        if k > 1:
            outgoing = call(hop_kernel(0), edge, [VMEM] * 4, VMEM, work // total)(
                got, y_high, y_low, backs
            )

    def last_kernel(in_ref, high_ref, low_ref, part_ref, mine_ref, other_ref, all_ref):
        for n in range(half):
            for e in range(total):
                all_ref[n, e] = part_ref[n, e] + rows(in_ref[n], high_ref[n, e], low_ref[n, e])
        first = core_index() * elems
        away = (1 - core_index()) * elems
        for n in range(half):
            for e in range(elems):
                mine_ref[n, e] = all_ref[n, first + e]
                other_ref[n, e] = all_ref[n, away + e]

    part = struct(half, elems, vecs, size)
    mine_z, other_z = call(
        last_kernel,
        (part, part),
        [VMEM] * 4,
        (VMEM,) * 2,
        work,
        scratch_shapes=[pltpu.VMEM(field.shape, F32)],
    )(incoming, y_high, y_low, backs)
    got_z = lax.ppermute(other_z, "axial", partner)

    face = proj_table.shape[1]
    wide = -(-face // 128) * 128
    groups = lax.axis_size("theta")
    crossings = intersection_list.shape[1]

    def trace_kernel(mine_ref, got_ref, out_ref, rows_ref):
        core = core_index()
        rows_ref[...] = jnp.zeros_like(rows_ref)
        for source, base in ((mine_ref, core * half), (got_ref, (1 - core) * half)):
            for n in range(half):
                at = pl.multiple_of((base + n) * vecs, vecs)
                rows_ref[pl.ds(at, vecs), :face] = source[n, elems - 1, :, size - face :]
        out_ref[...] = rows_ref[...].T[:face]

    traces = call(
        trace_kernel,
        struct(face, lines * vecs),
        [VMEM] * 2,
        VMEM,
        scratch_shapes=[pltpu.VMEM((lines * vecs, wide), F32)],
    )(mine_z, got_z)
    blocks = [traces]
    for s in range(1, groups):
        ring = [(t, t ^ s) for t in range(groups)]
        blocks.append(lax.ppermute(traces, "theta", ring))

    def join_kernel(mine_ref, got_ref, field_ref):
        core = core_index()
        for source, base in ((mine_ref, core * half), (got_ref, (1 - core) * half)):
            for n in range(half):
                field_ref[base + n] = source[n]

    solution = call(
        join_kernel, jax.ShapeDtypeStruct(rhs_field.shape, F32), [VMEM] * 2, VMEM
    )(mine_z, got_z)

    def mortar_kernel(list_ref, index_ref, angle_ref, table_ref, *rest):
        *block_refs, out_ref, rows_ref = rest
        here = lax.axis_index("theta")
        for s in range(groups):
            block = block_refs[s][...]
            if wide > face:
                block = jnp.concatenate(
                    [block, jnp.zeros((wide - face, lines * vecs), F32)], axis=0
                )
            rows_ref[s] = block.T
        for g in range(lines):
            sums = jnp.zeros((vecs, face), F32)
            for k in range(crossings):
                face_id = lax.rem(list_ref[g, k] + angle_ref[0], lines * groups)
                shift = lax.bitwise_xor(here, lax.div(face_id, lines))
                at = pl.multiple_of(lax.rem(face_id, lines) * vecs, vecs)
                trace = rows_ref[shift, pl.ds(at, vecs), :face]
                sums = sums + dot3(split(trace), split(table_ref[index_ref[g, k]]), RIGHT_T)
            out_ref[g] = sums

    mortar = call(
        mortar_kernel,
        jax.ShapeDtypeStruct((lines, vecs, face), F32),
        [SMEM] * 3 + [VMEM] * (1 + groups),
        VMEM,
        scratch_shapes=[pltpu.VMEM((groups, lines * vecs, wide), F32)],
    )(intersection_list, proj_index, angle_step, proj_table, *blocks)
    return (solution, mortar.reshape(1, lines, vecs * face))


def solution(mesh):
    block = P("theta", "axial", None, None)
    return jax.shard_map(
        local,
        mesh=mesh,
        in_specs=(block, block, block, block, P(), P("theta", None), P("theta", None), P()),
        out_specs=(block, P("axial", "theta", None)),
        check_vma=False,
    )
```

```python
import jax
import jax.numpy as jnp
from jax import lax
from jax.experimental import pallas as pl
from jax.experimental.pallas import tpu as pltpu
from jax.sharding import PartitionSpec as P


F32 = jnp.float32
BF16 = jnp.bfloat16
PLAIN = (((1,), (0,)), ((), ()))
RIGHT_T = (((1,), (1,)), ((), ()))
BOTH_T = (((0,), (1,)), ((), ()))
VMEM = pl.BlockSpec(memory_space=pltpu.VMEM)
SMEM = pl.BlockSpec(memory_space=pltpu.SMEM)
LIMIT = 12 << 20


def dot(a, b, dims=PLAIN):
    return lax.dot_general(a, b, dims, preferred_element_type=F32)


def split(a):
    high = a.astype(BF16)
    return high, (a - high.astype(F32)).astype(BF16)


def dot3(a, b, dims=PLAIN):
    ah, al = a
    bh, bl = b
    return dot(ah, bh, dims) + (dot(ah, bl, dims) + dot(al, bh, dims))


def rows(vectors, high, low):
    count = vectors.shape[0]
    vh, vl = split(vectors)
    both = dot(jnp.concatenate([vh, vl], axis=0), high)
    return both[:count] + (both[count:] + dot(vh, low))


def call(kernel, out_shape, in_specs, out_specs, flops=0, **kwargs):
    return pl.pallas_call(
        kernel,
        out_shape=out_shape,
        in_specs=in_specs,
        out_specs=out_specs,
        compiler_params=pltpu.CompilerParams(vmem_limit_bytes=LIMIT),
        cost_estimate=pl.CostEstimate(flops=flops, bytes_accessed=0, transcendentals=0),
        **kwargs,
    )


def struct(*shape, dtype=F32):
    return pltpu.VMEM(shape, dtype)


def product_of(left, right, left_stage, right_stage, slot):
    size, width = right.shape
    high, low = split(left)
    left_stage[slot, :, :size] = high
    left_stage[slot, :, size : 2 * size] = high
    left_stage[slot, :, 2 * size :] = low
    high, low = split(right)
    right_stage[slot, :size, :width] = high
    right_stage[slot, size : 2 * size, :width] = low
    right_stage[slot, 2 * size :, :width] = high
    return dot(right_stage[slot, :, :width], left_stage[slot], BOTH_T)


def stages(size, width):
    return [pltpu.VMEM((2, size, 3 * size), BF16), pltpu.VMEM((2, 3 * size, width), BF16)]


def products(left_ref, right_ref, rhs_ref, out_ref, out_g, left_stage, right_stage):
    half, elems, _, _ = left_ref.shape
    for n in range(half):
        for e in range(elems):
            slot = (n * elems + e) % 2
            out_ref[n, e] = -product_of(
                left_ref[n, e], right_ref[n, e], left_stage, right_stage, slot
            )
            high, low = split(rhs_ref[n, e])
            terms = jnp.concatenate([high, low, high], axis=1)
            out_g[n, e] = dot(terms, left_stage[slot], RIGHT_T)


def first_products(left, right, rhs, flops):
    lines, elems, size, _ = left.shape
    half = lines // 2
    vecs = rhs.shape[2]
    matrix = (half, elems, size, size)
    column = (half, elems, vecs, size)

    def kernel(
        left_hbm, right_hbm, rhs_hbm,
        out_ref, out_g, left_other, left_mine, right_mine, rhs_mine,
        right_other, rhs_other, left_stage, right_stage, sems,
    ):
        core = core_index()
        targets = ((left_other, right_other, rhs_other), (left_mine, right_mine, rhs_mine))
        near, far = (
            [
                pltpu.make_async_copy(
                    source.at[pl.ds(base * half, half)], target, sems.at[group, i]
                )
                for i, (source, target) in enumerate(zip((left_hbm, right_hbm, rhs_hbm), refs))
            ]
            for group, (base, refs) in enumerate(zip((1 - core, core), targets))
        )
        for copy in near + far:
            copy.start()
        for copy in near:
            copy.wait()
        products(left_other, right_other, rhs_other, out_ref, out_g, left_stage, right_stage)
        for copy in far:
            copy.wait()

    hbm = [pltpu.with_memory_space_constraint(x, pltpu.HBM) for x in (left, right, rhs)]
    return call(
        kernel,
        [struct(*shape) for shape in (matrix, column, matrix, matrix, matrix, column)],
        [pl.BlockSpec(memory_space=pltpu.HBM)] * 3,
        [VMEM] * 6,
        flops,
        scratch_shapes=[
            pltpu.VMEM(matrix, F32),
            pltpu.VMEM(column, F32),
            *stages(size, size),
            pltpu.SemaphoreType.DMA((2, 3)),
        ],
    )(*hbm)


def second_products(left, right, rhs, flops):
    size = left.shape[2]
    return call(
        products,
        [struct(*left.shape), struct(*rhs.shape)],
        [VMEM] * 3,
        [VMEM] * 2,
        flops,
        scratch_shapes=stages(size, size),
    )(left, right, rhs)


def late_products(left, right, flops):
    half, elems, size, _ = left.shape

    def kernel(left_ref, right_ref, out_ref, left_stage, right_stage):
        for n in range(half):
            for e in range(elems):
                slot = (n * elems + e) % 2
                out_ref[n, e] = -product_of(
                    left_ref[n, e], right_ref[n, e], left_stage, right_stage, slot
                )

    return call(
        kernel, struct(*left.shape), [VMEM] * 2, VMEM, flops, scratch_shapes=stages(size, size)
    )(left, right)


def stage_left(stage, n, start, count, high, low):
    size = high.shape[1]
    stage[n, start : start + count, :size] = high
    stage[n, start : start + count, size : 2 * size] = high
    stage[n, start : start + count, 2 * size :] = low


def stage_right(stage, n, high, low):
    size = high.shape[0]
    stage[n, :size] = high
    stage[n, size : 2 * size] = low
    stage[n, 2 * size :] = high


def composed(mine, got, order, flops, later=None):
    half, elems, size, _ = mine.shape

    def kernel(mine_ref, got_ref, *rest):
        copies = []
        if later is not None:
            later_hbm, *rest, sems = rest
            targets = rest[2:4]
            core = core_index()
            copies = [
                pltpu.make_async_copy(later_hbm.at[pl.ds(base * half, half)], target, sems.at[i])
                for i, (base, target) in enumerate(zip((1 - core, core), targets))
            ]
        out_high, out_low, *_, left_stage, right_stage = rest
        for copy in copies:
            copy.start()
        for n in range(half):
            first = pick(mine_ref, got_ref, n, order[0])
            out_high[n, order[0]], out_low[n, order[0]] = split(first)
        for before, e in zip(order, order[1:]):
            for n in range(half):
                stage_left(left_stage, n, 0, size, out_high[n, before], out_low[n, before])
                stage_right(right_stage, n, *split(pick(mine_ref, got_ref, n, e)))
                out_high[n, e], out_low[n, e] = split(dot(left_stage[n], right_stage[n]))
        for copy in copies:
            copy.wait()

    shapes = [struct(half, len(order), size, size, dtype=BF16)] * 2
    specs, operands = [VMEM] * 2, [mine, got]
    scratch = [
        pltpu.VMEM((half, size, 3 * size), BF16),
        pltpu.VMEM((half, 3 * size, size), BF16),
    ]
    if later is not None:
        shapes += [struct(half, elems, size, size)] * 2
        specs.append(pl.BlockSpec(memory_space=pltpu.HBM))
        operands.append(pltpu.with_memory_space_constraint(later, pltpu.HBM))
        scratch.append(pltpu.SemaphoreType.DMA((2,)))
    return call(
        kernel, shapes, specs, [VMEM] * len(shapes), flops, scratch_shapes=scratch
    )(*operands)


def turned(x_high, x_low, parts, mine, got, flops):
    half, total, size, _ = x_high.shape
    vecs = parts.shape[2]

    def kernel(
        xh_ref, xl_ref, part_ref, mine_ref, got_ref,
        out_high, out_low, out_part, left_stage, right_stage,
    ):
        last = total - 1

        @pl.when(lax.axis_index("axial") >= lax.axis_size("axial") - 2)
        def _():
            for n in range(half):
                out_high[n, last] = xh_ref[n, last]
                out_low[n, last] = xl_ref[n, last]
                out_part[n, last] = part_ref[n, last]
            for e in reversed(range(last)):
                for n in range(half):
                    stage_left(left_stage, n, 0, size, out_high[n, e + 1], out_low[n, e + 1])
                    stage_left(left_stage, n, size, vecs, *split(out_part[n, e + 1]))
                    stage_right(right_stage, n, *split(pick(mine_ref, got_ref, n, e)))
                    result = dot(left_stage[n], right_stage[n])
                    x = xh_ref[n, e].astype(F32) + xl_ref[n, e].astype(F32)
                    out_high[n, e], out_low[n, e] = split(x + result[:size])
                    out_part[n, e] = part_ref[n, e] + result[size:]

    shape = struct(*x_high.shape, dtype=BF16)
    return call(
        kernel,
        [shape, shape, struct(*parts.shape)],
        [VMEM] * 5,
        [VMEM] * 3,
        flops,
        scratch_shapes=[
            pltpu.VMEM((half, size + vecs, 3 * size), BF16),
            pltpu.VMEM((half, 3 * size, size), BF16),
        ],
    )(x_high, x_low, parts, mine, got)


def core_index():
    return lax.rem(lax.axis_index("axial"), 2)


def pick(mine_ref, got_ref, n, e):
    elems = mine_ref.shape[1]
    owner, place = divmod(e, elems)
    return jnp.where(core_index() == owner, mine_ref[n, place], got_ref[n, place])


def local(
    rhs_field,
    diag_inv,
    lower_block,
    upper_block,
    proj_table,
    intersection_list,
    proj_index,
    angle_step,
):
    lines, elems, vecs, size = rhs_field.shape
    devices = lax.axis_size("axial")
    chips = devices // 2
    half = lines // 2
    total = 2 * elems
    partner = [(d, d ^ 1) for d in range(devices)]
    field = struct(half, total, vecs, size)
    edge = struct(half, vecs, size)
    work = half * total * 6 * vecs * size**2

    heavy = half * elems * 6 * size**3
    other_p, other_g, d_other, d_mine, l_mine, r_mine = first_products(
        diag_inv, lower_block, rhs_field, heavy
    )
    got_p = lax.ppermute(other_p, "axial", partner)
    got_g = lax.ppermute(other_g, "axial", partner)
    mine_p, mine_g = second_products(d_mine, l_mine, r_mine, heavy)

    def start_kernel(mine_ref, got_ref, mine_g_ref, got_g_ref, part_ref):
        for n in range(half):
            current = pick(mine_g_ref, got_g_ref, n, 0)
            part_ref[n, 0] = current
            for e in range(1, total):
                operator = split(pick(mine_ref, got_ref, n, e))
                current = pick(mine_g_ref, got_g_ref, n, e) + rows(current, *operator)
                part_ref[n, e] = current

    parts = call(start_kernel, field, [VMEM] * 4, VMEM, work)(mine_p, got_p, mine_g, got_g)
    outgoing = parts[:, -1]

    x_high, x_low, u_other, u_mine = composed(
        mine_p, got_p, list(range(total)), 2 * heavy, upper_block
    )

    def hop_kernel(edge_at):
        def kernel(in_ref, high_ref, low_ref, part_ref, out_ref):
            for n in range(half):
                out_ref[n] = part_ref[n, edge_at] + rows(
                    in_ref[n], high_ref[n, edge_at], low_ref[n, edge_at]
                )

        return kernel

    incoming = jnp.zeros_like(outgoing)
    for k in range(chips - 1):
        got = lax.ppermute(outgoing, "axial", [(2 * k + c, 2 * k + 2 + c) for c in range(2)])
        incoming = incoming + got
        if k < chips - 2:
            outgoing = call(hop_kernel(total - 1), edge, [VMEM] * 4, VMEM, work // total)(
                got, x_high, x_low, parts
            )

    other_q = late_products(d_other, u_other, heavy)
    got_q = lax.ppermute(other_q, "axial", partner)
    mine_q = late_products(d_mine, u_mine, heavy)

    t_high, t_low, t_parts = turned(x_high, x_low, parts, mine_q, got_q, 2 * heavy)

    def turn_kernel(*refs):
        @pl.when(lax.axis_index("axial") >= devices - 2)
        def _():
            hop_kernel(0)(*refs)

    outgoing = call(turn_kernel, edge, [VMEM] * 4, VMEM, work // total)(
        incoming, t_high, t_low, t_parts
    )

    def back_kernel(in_ref, high_ref, low_ref, part_ref, mine_ref, got_ref, out_ref):
        for n in range(half):
            for e in range(total):
                out_ref[n, e] = part_ref[n, e] + rows(in_ref[n], high_ref[n, e], low_ref[n, e])
        for n in range(half):
            current = out_ref[n, total - 1]
            for e in reversed(range(total - 1)):
                operator = split(pick(mine_ref, got_ref, n, e))
                current = out_ref[n, e] + rows(current, *operator)
                out_ref[n, e] = current

    backs = call(back_kernel, field, [VMEM] * 6, VMEM, 2 * work)(
        incoming, x_high, x_low, parts, mine_q, got_q
    )
    y_high, y_low = composed(mine_q, got_q, list(range(total))[::-1], 2 * heavy)

    incoming = jnp.zeros_like(outgoing)
    for k in reversed(range(1, chips)):
        got = lax.ppermute(outgoing, "axial", [(2 * k + c, 2 * k - 2 + c) for c in range(2)])
        incoming = incoming + got
        if k > 1:
            outgoing = call(hop_kernel(0), edge, [VMEM] * 4, VMEM, work // total)(
                got, y_high, y_low, backs
            )

    def last_kernel(in_ref, high_ref, low_ref, part_ref, mine_ref, other_ref, all_ref):
        for n in range(half):
            for e in range(total):
                all_ref[n, e] = part_ref[n, e] + rows(in_ref[n], high_ref[n, e], low_ref[n, e])
        first = core_index() * elems
        away = (1 - core_index()) * elems
        for n in range(half):
            for e in range(elems):
                mine_ref[n, e] = all_ref[n, first + e]
                other_ref[n, e] = all_ref[n, away + e]

    part = struct(half, elems, vecs, size)
    mine_z, other_z = call(
        last_kernel,
        (part, part),
        [VMEM] * 4,
        (VMEM,) * 2,
        work,
        scratch_shapes=[pltpu.VMEM(field.shape, F32)],
    )(incoming, y_high, y_low, backs)
    got_z = lax.ppermute(other_z, "axial", partner)

    face = proj_table.shape[1]
    wide = -(-face // 128) * 128
    groups = lax.axis_size("theta")
    crossings = intersection_list.shape[1]

    def trace_kernel(mine_ref, got_ref, out_ref, rows_ref):
        core = core_index()
        rows_ref[...] = jnp.zeros_like(rows_ref)
        for source, base in ((mine_ref, core * half), (got_ref, (1 - core) * half)):
            for n in range(half):
                at = pl.multiple_of((base + n) * vecs, vecs)
                rows_ref[pl.ds(at, vecs), :face] = source[n, elems - 1, :, size - face :]
        out_ref[...] = rows_ref[...].T[:face]

    traces = call(
        trace_kernel,
        struct(face, lines * vecs),
        [VMEM] * 2,
        VMEM,
        scratch_shapes=[pltpu.VMEM((lines * vecs, wide), F32)],
    )(mine_z, got_z)
    blocks = [traces]
    for s in range(1, groups):
        ring = [(t, t ^ s) for t in range(groups)]
        blocks.append(lax.ppermute(traces, "theta", ring))

    def join_kernel(mine_ref, got_ref, field_ref):
        core = core_index()
        for source, base in ((mine_ref, core * half), (got_ref, (1 - core) * half)):
            for n in range(half):
                field_ref[base + n] = source[n]

    solution = call(
        join_kernel, jax.ShapeDtypeStruct(rhs_field.shape, F32), [VMEM] * 2, VMEM
    )(mine_z, got_z)

    def mortar_kernel(list_ref, index_ref, angle_ref, table_ref, *rest):
        *block_refs, out_ref, rows_ref = rest
        here = lax.axis_index("theta")
        for s in range(groups):
            block = block_refs[s][...]
            if wide > face:
                block = jnp.concatenate(
                    [block, jnp.zeros((wide - face, lines * vecs), F32)], axis=0
                )
            rows_ref[s] = block.T
        for g in range(lines):
            sums = jnp.zeros((vecs, face), F32)
            for k in range(crossings):
                face_id = lax.rem(list_ref[g, k] + angle_ref[0], lines * groups)
                shift = lax.bitwise_xor(here, lax.div(face_id, lines))
                at = pl.multiple_of(lax.rem(face_id, lines) * vecs, vecs)
                trace = rows_ref[shift, pl.ds(at, vecs), :face]
                sums = sums + dot3(split(trace), split(table_ref[index_ref[g, k]]), RIGHT_T)
            out_ref[g] = sums

    mortar = call(
        mortar_kernel,
        jax.ShapeDtypeStruct((lines, vecs, face), F32),
        [SMEM] * 3 + [VMEM] * (1 + groups),
        VMEM,
        scratch_shapes=[pltpu.VMEM((groups, lines * vecs, wide), F32)],
    )(intersection_list, proj_index, angle_step, proj_table, *blocks)
    return (solution, mortar.reshape(1, lines, vecs * face))


def solution(mesh):
    block = P("theta", "axial", None, None)
    return jax.shard_map(
        local,
        mesh=mesh,
        in_specs=(block, block, block, block, P(), P("theta", None), P("theta", None), P()),
        out_specs=(block, P("axial", "theta", None)),
        check_vma=False,
    )
```
